32 devices in a mesh: grp: 1, pool: 1, ep: 8 (over z, y), tp: 4 (over x, core).
Axes of the slice: x: 2, y: 2, z: 4, core: 2. Of those that a mesh axis runs over, the one named last changes fastest.
Arguments:
- queries: bfloat16 [1024, 4096], P(('grp', 'ep'), ('pool', 'tp')), may hold values from -6 to 6
- keys_values: bfloat16 [1024, 1024], P(('grp', 'ep'), 'pool'), may hold values from -6 to 6
- residual: bfloat16 [1024, 2048], P(('grp', 'ep', 'tp'), 'pool'), may hold values from -24 to 24
- norm_gain: float32 [2048], P('pool'), may hold values from 0.1 to 1.9
- w_out: bfloat16 [4096, 2048], P(('pool', 'tp')), may hold values from -0.75 to 0.75
- w_gate_up: bfloat16 [32, 2048, 768], P(('ep', 'tp'), 'pool'), may hold values from -0.125 to 0.125
- w_down: bfloat16 [32, 384, 2048], P(('ep', 'tp'), None, 'pool'), may hold values from -0.3125 to 0.3125
- expert_ids: int32 [1024, 8], P(('grp', 'ep', 'tp')), may hold values from 0 to 31, as said below
- mix_weights: float32 [1024, 8], P(('grp', 'ep', 'tp')), may hold values from 0.1 to 1
- clip_lengths: int32 [3], P('grp'), may hold values from 129 to 512, as said below
Outputs:
- layer_out: bfloat16 [1024, 2048], P(('grp', 'ep', 'tp'), 'pool')
The draws below stay inside these ranges and needn't reach their ends.
Inputs may be any that keep to these rules, and one draw needn't show every extreme that they name: `clip_lengths`: 3 clips cover the 1024 tokens; one clip has exactly 512 tokens. `expert_ids`: each row names 8 different experts. Among the 32 rows of one device (aligned blocks of rows) no expert is named more than 16 times, and one expert is named exactly 16 times in every block.
All inputs are finite; a program needn't handle non-finite values.
Results may differ from the reference program's by a relative error of at most 0.018.
Values may be sent and summed in bfloat16 or wider, within the bound.
No kernel may reach another device: no remote copies, remote signals or barrier semaphores. Data moves between devices by JAX's collectives and lax.ppermute only.
A program may use at most 64 MiB of HBM per device.

```python
import math
import jax
import jax.numpy as jnp
from jax import lax

D = 2048
QH = 32
KVH = 4
HD = 128
FF = 384
TOP = 8
TOKENS = 1024
CLIP = 512
EXPERTS = 32
GROUP_ROWS = 32
CAP = 16
HEAD_SETS = 4
SET_HEADS = 8
N_EP = 8
N_TP = 4


def draw_queries(key, part):
    drawn = jax.random.normal(jax.random.fold_in(key, 11), (TOKENS, QH * HD), jnp.float32)
    return jnp.clip(1.4 * drawn, -6.0, 6.0).astype(jnp.bfloat16)


def draw_keys_values(key, part):
    drawn = jax.random.normal(jax.random.fold_in(key, 21), (TOKENS, KVH * 2 * HD), jnp.float32)
    return jnp.clip(1.4 * drawn, -6.0, 6.0).astype(jnp.bfloat16)


def draw_residual(key, part):
    columns = jnp.arange(D, dtype=jnp.float32) / D
    rough = jnp.exp(jax.random.uniform(jax.random.fold_in(key, 52), (D,), jnp.float32, -0.3567, 0.3365))
    drawn = jax.random.normal(jax.random.fold_in(key, 51), (TOKENS, D), jnp.float32)
    rise = 3.0 ** (2.0 * columns - 1.0)
    values = jnp.clip(drawn, -4.0, 4.0) * rise[None, :] * rough[None, :]
    return jnp.clip(values, -24.0, 24.0).astype(jnp.bfloat16)


def draw_clip_lengths(key, part):
    count = TOKENS // CLIP
    rest = TOKENS - CLIP
    base = rest // count
    shifts = jax.random.randint(jax.random.fold_in(key, 31), (count,), 0, CLIP // 4)
    others = base + shifts - jnp.roll(shifts, 1)
    others = others.at[0].add(rest - base * count)
    where = jax.random.randint(jax.random.fold_in(key, 32), (), 0, count + 1)
    positions = jnp.arange(count + 1, dtype=jnp.int32)
    source = jnp.where(positions < where, positions, positions - 1)
    picked = others[jnp.clip(source, 0, count - 1)]
    return jnp.where(positions == where, CLIP, picked).astype(jnp.int32)


def permute_experts(one_key):
    return jax.random.permutation(one_key, EXPERTS)


def draw_expert_ids(key, part):
    blocks = TOKENS // GROUP_ROWS
    pairs = EXPERTS // 2
    order_all = jax.random.permutation(jax.random.fold_in(key, 41), EXPERTS).astype(jnp.int32)
    bias = jax.random.randint(jax.random.fold_in(key, 42), (1, pairs), 0, CAP + 1)
    noise = jax.random.randint(jax.random.fold_in(key, 43), (blocks, pairs), -(CAP // 2), CAP // 2 + 1)
    first = jnp.clip(bias + noise, 0, CAP)
    spare = jax.random.randint(jax.random.fold_in(key, 44), (blocks,), 0, CAP + 1)
    share = jax.random.randint(jax.random.fold_in(key, 45), (blocks,), 0, CAP + 1)
    second = CAP - first
    first = first.at[:, 0].set(CAP)
    second = second.at[:, 0].set(spare)
    split = (CAP - spare) * share // CAP
    first = first.at[:, 1].set(split)
    second = second.at[:, 1].set(CAP - spare - split)
    counts = jnp.zeros((blocks, EXPERTS), jnp.int32)
    counts = counts.at[:, order_all[0::2]].set(first).at[:, order_all[1::2]].set(second)
    orders = jax.vmap(permute_experts)(jax.random.split(jax.random.fold_in(key, 46), blocks)).astype(jnp.int32)
    ordered = jnp.take_along_axis(counts, orders, axis=1)
    ends = jnp.cumsum(ordered, axis=1)
    places = jnp.arange(GROUP_ROWS * TOP, dtype=jnp.int32)
    which = jnp.sum((ends[:, None, :] <= places[None, :, None]).astype(jnp.int32), axis=2)
    sequence = jnp.take_along_axis(orders, which, axis=1)
    return sequence.reshape(blocks, TOP, GROUP_ROWS).transpose(0, 2, 1).reshape(TOKENS, TOP).astype(jnp.int32)


def with_spikes(drawn, stream_key, source, target, blocks, factor):
    owner, partner = [(jnp.arange(drawn.shape[dim]) // (drawn.shape[dim] // blocks)).reshape([-1 if axis == dim else 1 for axis in range(drawn.ndim)]) for dim in (source, target)]
    chosen = jax.random.permutation(stream_key, blocks)[partner]
    strong = (owner == chosen) | (owner == (partner + blocks // 2) % blocks)
    return jnp.where(strong, factor * drawn, drawn)


def level_of(own_key, dims, shards, smallest, top_value):
    level = 1.0
    for position, shards_of in shards:
        steps = jax.random.uniform(jax.random.fold_in(jax.random.fold_in(own_key, 6), position), (shards_of,), jnp.float32, smallest / len(shards), top_value / len(shards))
        level = level * jnp.repeat(jnp.exp(steps), dims[position] // shards_of).reshape((-1,) + (1,) * (len(dims) - 1 - position))
    return level


def gaussian(key, dims, deviation, reach, shards=(), kind=jnp.bfloat16):
    level = level_of(key, dims, shards, -0.22, 0.18) if shards else 1.0
    drawn = jax.random.normal(key, dims, jnp.float32) * deviation * level
    return jnp.minimum(jnp.maximum(drawn, -reach), reach).astype(kind)


def gaussian_with(own_key, extent, width, bound, pieces, heavy, held_as=jnp.bfloat16):
    values = width * jax.random.normal(own_key, extent, jnp.float32)
    if pieces:
        values = values * level_of(own_key, extent, pieces, -0.22, 0.18)
    return jnp.clip(with_spikes(values, jax.random.fold_in(own_key, 3), *heavy), -bound, bound).astype(held_as)


def setup_inputs(seed: int = 0, part: int = 0) -> dict:
    splits = jax.random.split(jax.random.key(seed), 11)
    own_keys = jax.random.split(jax.random.fold_in(splits[10], part), 11)
    return {
        "queries": draw_queries(jax.random.fold_in(jax.random.fold_in(splits[10], part), 71), part),
        "keys_values": draw_keys_values(jax.random.fold_in(jax.random.fold_in(splits[10], part), 71), part),
        "residual": draw_residual(jax.random.fold_in(jax.random.fold_in(splits[10], part), 71), part),
        "norm_gain": jnp.clip(1.0 + 0.18 * jax.random.normal(splits[3], (D,), jnp.float32), 0.1, 1.9),
        "w_out": gaussian_with(splits[4], (QH * HD, D), HD ** -0.5, 0.75, ((0, 4),), (0, 1, 4, 2.0)),
        "w_gate_up": gaussian(splits[5], (EXPERTS, D, 2 * FF), D ** -0.5, 0.125, ((0, 32),)),
        "w_down": gaussian(splits[6], (EXPERTS, FF, D), FF ** -0.5, 0.3125, ((0, 32),)),
        "expert_ids": draw_expert_ids(jax.random.fold_in(jax.random.fold_in(splits[10], part), 71), part),
        "mix_weights": jnp.clip(jnp.exp(math.log(1.0) - 2.3025851 * jax.random.uniform(own_keys[8], (TOKENS, TOP), jnp.float32) ** level_of(own_keys[8], (TOKENS, TOP), ((0, 32),), -0.2, 0.2)), 0.1, 1.0),
        "clip_lengths": draw_clip_lengths(jax.random.fold_in(jax.random.fold_in(splits[10], part), 71), part),
    }


def clip_index(clip_lengths, count):
    ends = jnp.cumsum(clip_lengths)
    places = jnp.arange(count, dtype=jnp.int32)
    return lax.optimization_barrier(jnp.sum((places[:, None] >= ends[None, :]).astype(jnp.int32), axis=1))

def attend_head(query, keys, values, clips_of):
    scores = jnp.dot(query.astype(jnp.float32), keys.astype(jnp.float32).T) * HD ** (-0.5)
    same = clips_of[:, None] == clips_of[None, :]
    masked = jnp.where(same, scores, -1e+30)
    top = lax.optimization_barrier(jnp.max(masked, axis=1, keepdims=True))
    weights = jnp.where(same, jnp.exp(masked - top), 0.0)
    denom = lax.optimization_barrier(jnp.sum(weights, axis=1, keepdims=True))
    probs = weights.astype(jnp.bfloat16)
    numer = jnp.dot(probs.astype(jnp.float32), values.astype(jnp.float32))
    return (numer / denom).astype(jnp.bfloat16)

def reference(queries, keys_values, residual, norm_gain, w_out, w_gate_up, w_down, expert_ids, mix_weights, clip_lengths):
    clips_of = clip_index(clip_lengths, TOKENS)
    group = QH // KVH

    def one_head(head):
        query = lax.dynamic_slice_in_dim(queries, head * HD, HD, 1)
        base = head // group * (2 * HD)
        keys = lax.dynamic_slice_in_dim(keys_values, base, HD, 1)
        values = lax.dynamic_slice_in_dim(keys_values, base + HD, HD, 1)
        return attend_head(query, keys, values, clips_of)
    heads = lax.map(one_head, jnp.arange(QH, dtype=jnp.int32))
    head_sets = heads.reshape(HEAD_SETS, SET_HEADS, TOKENS, HD)
    weight_sets = w_out.reshape(HEAD_SETS, SET_HEADS, HD, D)

    def add_set(total, pair):
        part_heads, part_weights = pair
        term = jnp.einsum('htd,hde->te', part_heads.astype(jnp.float32), part_weights.astype(jnp.float32))
        rounded = lax.optimization_barrier(term.astype(jnp.bfloat16))
        return (total + rounded.astype(jnp.float32), None)
    attn_sum, _ = lax.scan(add_set, jnp.zeros((TOKENS, D), jnp.float32), (head_sets, weight_sets))
    hidden_state = residual.astype(jnp.float32) + attn_sum
    mean_square = lax.optimization_barrier(jnp.mean(hidden_state * hidden_state, axis=1))
    normed = (hidden_state * lax.rsqrt(mean_square + 1e-06)[:, None] * norm_gain[None, :]).astype(jnp.bfloat16)
    flat = expert_ids.reshape(-1)
    order = jnp.argsort(flat, stable=True).astype(jnp.int32)
    counts = lax.optimization_barrier(jnp.sum((flat[:, None] == jnp.arange(EXPERTS, dtype=jnp.int32)[None, :]).astype(jnp.int32), axis=0))
    starts = jnp.cumsum(counts) - counts
    most = N_EP * N_TP * CAP
    slots = jnp.arange(most, dtype=jnp.int32)
    assigned = TOKENS * TOP

    def run_expert(carry, expert):
        place = starts[expert] + slots
        valid = slots < counts[expert]
        pick = order[jnp.minimum(place, assigned - 1)]
        chosen = normed[pick // TOP]
        both = jnp.dot(chosen.astype(jnp.float32), w_gate_up[expert].astype(jnp.float32))
        hidden = (jax.nn.silu(both[:, :FF]) * both[:, FF:]).astype(jnp.bfloat16)
        result = jnp.dot(hidden.astype(jnp.float32), w_down[expert].astype(jnp.float32)).astype(jnp.bfloat16)
        target = jnp.where(valid, pick, assigned)
        return (carry.at[target].set(result, mode='drop'), None)
    outputs, _ = lax.scan(run_expert, jnp.zeros((assigned, D), jnp.bfloat16), jnp.arange(EXPERTS, dtype=jnp.int32))
    blended = jnp.einsum('tkd,tk->td', outputs.reshape(TOKENS, TOP, D).astype(jnp.float32), mix_weights.astype(jnp.float32))
    return (hidden_state + blended).astype(jnp.bfloat16)
```

```python
import functools
import jax
import jax.numpy as jnp
from jax import lax
from jax.experimental import pallas as pl
from jax.experimental.pallas import tpu as pltpu
from jax.sharding import PartitionSpec as P

D = 2048
QH = 32
KVH = 4
HD = 128
LANES = 128


def halves(size):
    return (size // 2, 2) if size % 2 == 0 else (size, 1)


def shift_pairs(sizes, dim, step):
    total = 1
    for size in sizes:
        total *= size
    stride = 1
    for size in sizes[dim + 1 :]:
        stride *= size
    pairs = []
    for source in range(total):
        at = source // stride % sizes[dim]
        pairs.append((source, source + ((at + step) % sizes[dim] - at) * stride))
    return pairs


def attend_kernel(
    hs, lengths, nclips, slots, moe_rows, info_ref, q_ref, *refs
):
    nkv = len(lengths)
    kv_refs = refs[:nkv]
    w_ref = refs[nkv]
    out_refs = refs[nkv + 1 : nkv + 1 + slots]
    acc_ref, bias_ref = refs[nkv + 1 + slots :]
    rows = q_ref.shape[0]
    step = pl.program_id(0)
    block = rows

    def clip_at(places):
        clip = jnp.zeros_like(places)
        for index in range(nclips):
            clip = clip + jnp.where(places >= info_ref[index], 1, 0)
        return clip

    @pl.when(step == 0)
    def _():
        acc_ref[...] = jnp.zeros_like(acc_ref)
        q_clip = clip_at(info_ref[nclips] + lax.broadcasted_iota(jnp.int32, (rows, block), 0))
        for index in range(sum(lengths) // block):
            k_clip = clip_at(
                info_ref[nclips + 2 + index]
                + lax.broadcasted_iota(jnp.int32, (rows, block), 1)
            )
            bias_ref[:, index * block : (index + 1) * block] = jnp.where(
                q_clip == k_clip, 0.0, -1e30
            )

    query = jnp.concatenate([q_ref[:, h * HD : (h + 1) * HD] for h in range(hs)], axis=0)
    scores = []
    at = 0
    for ref, length in zip(kv_refs, lengths):
        part = lax.dot_general(
            query, ref[:, :HD], (((1,), (1,)), ((), ())), preferred_element_type=jnp.float32
        )
        bias = bias_ref[:, at : at + length]
        scores.append(part * HD ** (-0.5) + jnp.concatenate([bias] * hs, axis=0))
        at += length
    top = functools.reduce(
        jnp.maximum, [jnp.max(part, axis=1, keepdims=True) for part in scores]
    )
    total = 0.0
    numer = 0.0
    for ref, part in zip(kv_refs, scores):
        weights = jnp.exp(part - top)
        total = total + jnp.sum(weights, axis=1, keepdims=True)
        numer = numer + jnp.dot(
            weights.astype(jnp.bfloat16), ref[:, HD:], preferred_element_type=jnp.float32
        )
    attended = (numer / total).astype(jnp.bfloat16)
    wide = jnp.concatenate([attended[h * rows : (h + 1) * rows] for h in range(hs)], axis=1)
    acc_ref[...] += jnp.dot(wide, w_ref[...], preferred_element_type=jnp.float32)

    @pl.when(step == pl.num_programs(0) - 1)
    def _():
        half = out_refs[0].shape[1]
        parts = acc_ref.shape[1] // half
        tensor = slots // parts
        me = info_ref[nclips + 1]
        for slot in range(slots):
            to = lax.rem(me + slot, slots)
            row = pl.multiple_of(lax.rem(to, tensor) * moe_rows, moe_rows)
            if parts == 1:
                piece = acc_ref[pl.ds(row, moe_rows), :]
            else:
                column = pl.multiple_of(to // tensor * half, half)
                piece = acc_ref[pl.ds(row, moe_rows), pl.ds(column, half)]
            out_refs[slot][...] = piece.astype(out_refs[slot].dtype)


def attend(info, queries, kv_parts, w_out, nclips, slots, moe_rows, half):
    rows = queries.shape[0]
    heads = queries.shape[1] // HD
    hs = 2 if heads % 2 == 0 else 1
    lengths = tuple(part.shape[0] for part in kv_parts)
    whole = lambda g, info: (0, 0)
    return pl.pallas_call(
        functools.partial(attend_kernel, hs, lengths, nclips, slots, moe_rows),
        out_shape=[jax.ShapeDtypeStruct((moe_rows, half), jnp.bfloat16)] * slots,
        grid_spec=pltpu.PrefetchScalarGridSpec(
            num_scalar_prefetch=1,
            grid=(heads // hs,),
            in_specs=[pl.BlockSpec((rows, hs * HD), lambda g, info: (0, g))]
            + [pl.BlockSpec(part.shape, whole) for part in kv_parts]
            + [pl.BlockSpec((hs * HD, w_out.shape[1]), lambda g, info: (g, 0))],
            out_specs=[pl.BlockSpec((moe_rows, half), whole)] * slots,
            scratch_shapes=[
                pltpu.VMEM((rows, w_out.shape[1]), jnp.float32),
                pltpu.VMEM((rows, sum(lengths)), jnp.float32),
            ],
        ),
        name="attend",
    )(info, queries, *kv_parts, w_out)


def body(
    queries,
    keys_values,
    residual,
    norm_gain,
    w_out,
    w_gate_up,
    w_down,
    expert_ids,
    mix_weights,
    clip_lengths,
):
    rows = queries.shape[0]
    heads_here = queries.shape[1] // HD
    moe_rows, half = residual.shape
    pool_size, tensor_size, context_size = (lax.axis_size(a) for a in ("pool", "tp", "ep"))
    pool_index, tensor_index, context_index = (lax.axis_index(a) for a in ("pool", "tp", "ep"))
    outer, inner = halves(context_size)
    tall, near = halves(tensor_size)
    sizes = (outer, inner, tall, near)
    mesh_axes = ("ep", "tp")

    def moved(value, dim, step, keep=None):
        pairs = shift_pairs(sizes, dim, step)
        if keep is not None:
            pairs = [pair for pair in pairs if keep(*pair)]
        return lax.ppermute(value, mesh_axes, pairs)

    pair_heads = keys_values.shape[1] // (2 * HD)
    head_pick = (
        pool_index * tensor_size + tensor_index
    ) * heads_here // (QH // KVH) - pool_index * pair_heads
    own_pairs = lax.dynamic_slice_in_dim(keys_values, head_pick * (2 * HD), 2 * HD, 1)
    longest = context_size * rows // 2

    def in_reach(source, target):
        apart = abs(source // (inner * tensor_size) - target // (inner * tensor_size))
        nearest = apart * inner - (inner - 1)
        return (nearest - 1) * rows + 1 < longest

    near_parts = [own_pairs]
    for step in range(1, outer):
        near_parts.append(moved(own_pairs, 0, -step, in_reach))
    kv_parts = [jnp.concatenate(near_parts, axis=0)]
    for step in range(1, inner):
        kv_parts.append(moved(kv_parts[0], 1, -step))
    outer_index, inner_index = context_index // inner, context_index % inner
    bases = [
        (((outer_index + a) % outer) * inner + (inner_index + b) % inner) * rows
        for b in range(inner)
        for a in range(outer)
    ]
    ends = jnp.cumsum(clip_lengths)
    slots = pool_size * tensor_size
    shard = pool_index * tensor_size + tensor_index
    info = jnp.concatenate(
        [ends, jnp.stack([context_index * rows, shard] + bases)]
    ).astype(jnp.int32)
    terms = attend(info, queries, kv_parts, w_out, ends.shape[0], slots, moe_rows, half)

    mixed = terms[0].astype(jnp.float32)
    for step in range(1, slots):
        pairs = [(source, (source + step) % slots) for source in range(slots)]
        mixed = mixed + lax.ppermute(terms[step], ("pool", "tp"), pairs).astype(jnp.float32)
    hidden_state = residual.astype(jnp.float32) + mixed
    squares = jnp.sum(hidden_state * hidden_state, axis=1)
    if pool_size > 1:
        squares = lax.psum(squares, "pool")
    normed = (hidden_state * lax.rsqrt(squares / D + 1e-06)[:, None] * norm_gain[None, :]).astype(
        jnp.bfloat16
    )

    local_experts = w_gate_up.shape[0]
    experts = local_experts * context_size * tensor_size
    marks = expert_ids[:, :, None] == jnp.arange(experts, dtype=jnp.int32)[None, None, :]
    share = jnp.sum(jnp.where(marks, mix_weights[:, :, None], 0.0), axis=1)
    high = lax.reduce_precision(share, 8, 7)
    width = -(-2 * experts // LANES) * LANES
    tail = jnp.concatenate(
        [high, share - high, jnp.zeros((moe_rows, width - 2 * experts), jnp.float32)], axis=1
    ).astype(jnp.bfloat16)
    packet = jnp.concatenate([normed, tail], axis=1)

    def gather(value, dim):
        return jnp.concatenate(
            [value] + [moved(value, dim, -step) for step in range(1, sizes[dim])], axis=0
        )

    def fold(value, dim):
        count = value.shape[0] // sizes[dim]
        total = value[:count].astype(jnp.float32)
        for step in range(1, sizes[dim]):
            piece = value[step * count : (step + 1) * count]
            total = total + moved(piece, dim, step).astype(jnp.float32)
        return total.astype(jnp.bfloat16)

    cut = moe_rows // 2
    halves_of = [packet[:cut], packet[cut:]]
    orders = [(0, 2, 1, 3), (0, 1, 2, 3)]
    results = []
    own = (context_index * tensor_size + tensor_index) * local_experts
    for value, order in zip(halves_of, orders):
        for dim in order:
            value = gather(value, dim)
        tokens = value[:, :half]
        shares = value[:, half:].astype(jnp.float32)
        blended = 0.0
        for index in range(local_experts):
            both = jnp.dot(tokens, w_gate_up[index], preferred_element_type=jnp.float32)
            if pool_size > 1:
                both = lax.psum(both.astype(jnp.bfloat16), "pool").astype(jnp.float32)
            ff = w_down.shape[1]
            hidden = (jax.nn.silu(both[:, :ff]) * both[:, ff:]).astype(jnp.bfloat16)
            lane = lax.broadcasted_iota(jnp.int32, (1, width), 1)
            chosen = (lane == own + index) | (lane == own + index + experts)
            weight = jnp.sum(jnp.where(chosen, shares, 0.0), axis=1, keepdims=True)
            out = jnp.dot(hidden, w_down[index], preferred_element_type=jnp.float32)
            blended = blended + out * weight
        value = blended.astype(jnp.bfloat16)
        for dim in reversed(order):
            value = fold(value, dim)
        results.append(value)
    blend = jnp.concatenate(results, axis=0).astype(jnp.float32)
    return (hidden_state + blend).astype(jnp.bfloat16)


def solution(mesh):
    placed = (
        P(("grp", "ep"), ("pool", "tp")),
        P(("grp", "ep"), "pool"),
        P(("grp", "ep", "tp"), "pool"),
        P("pool"),
        P(("pool", "tp"), None),
        P(("ep", "tp"), "pool", None),
        P(("ep", "tp"), None, "pool"),
        P(("grp", "ep", "tp"), None),
        P(("grp", "ep", "tp"), None),
        P("grp"),
    )
    return jax.shard_map(
        body, mesh=mesh, in_specs=placed, out_specs=P(("grp", "ep", "tp"), "pool"), check_vma=False
    )
```

```python
import functools
import jax
import jax.numpy as jnp
from jax import lax
from jax.experimental import pallas as pl
from jax.experimental.pallas import tpu as pltpu
from jax.sharding import PartitionSpec as P

D = 2048
QH = 32
KVH = 4
HD = 128
LANES = 128
CHUNKS = 2
SMALL = pltpu.CompilerParams(vmem_limit_bytes=8 << 20)
LARGE = pltpu.CompilerParams(vmem_limit_bytes=40 << 20)


def halves(size):
    return (size // 2, 2) if size % 2 == 0 else (size, 1)


def shift_pairs(sizes, dim, step):
    total = 1
    for size in sizes:
        total *= size
    stride = 1
    for size in sizes[dim + 1 :]:
        stride *= size
    pairs = []
    for source in range(total):
        at = source // stride % sizes[dim]
        pairs.append((source, source + ((at + step) % sizes[dim] - at) * stride))
    return pairs


def attend_kernel(
    hs, lengths, nclips, slots, moe_rows, info_ref, q_ref, *refs
):
    nkv = len(lengths)
    kv_refs = refs[:nkv]
    w_ref = refs[nkv]
    out_refs = refs[nkv + 1 : nkv + 1 + slots]
    acc_ref, bias_ref = refs[nkv + 1 + slots :]
    rows = q_ref.shape[0]
    step = pl.program_id(0)
    block = rows

    def clip_at(places):
        clip = jnp.zeros_like(places)
        for index in range(nclips):
            clip = clip + jnp.where(places >= info_ref[index], 1, 0)
        return clip

    @pl.when(step == 0)
    def _():
        acc_ref[...] = jnp.zeros_like(acc_ref)
        q_clip = clip_at(info_ref[nclips] + lax.broadcasted_iota(jnp.int32, (rows, block), 0))
        for index in range(sum(lengths) // block):
            k_clip = clip_at(
                info_ref[nclips + 2 + index]
                + lax.broadcasted_iota(jnp.int32, (rows, block), 1)
            )
            bias_ref[:, index * block : (index + 1) * block] = jnp.where(
                q_clip == k_clip, 0.0, -1e30
            )

    query = jnp.concatenate([q_ref[:, h * HD : (h + 1) * HD] for h in range(hs)], axis=0)
    scores = []
    at = 0
    for ref, length in zip(kv_refs, lengths):
        part = lax.dot_general(
            query, ref[:, :HD], (((1,), (1,)), ((), ())), preferred_element_type=jnp.float32
        )
        bias = bias_ref[:, at : at + length]
        scores.append(part * HD ** (-0.5) + jnp.concatenate([bias] * hs, axis=0))
        at += length
    top = functools.reduce(
        jnp.maximum, [jnp.max(part, axis=1, keepdims=True) for part in scores]
    )
    total = 0.0
    numer = 0.0
    for ref, part in zip(kv_refs, scores):
        weights = jnp.exp(part - top)
        total = total + jnp.sum(weights, axis=1, keepdims=True)
        numer = numer + jnp.dot(
            weights.astype(jnp.bfloat16), ref[:, HD:], preferred_element_type=jnp.float32
        )
    attended = (numer / total).astype(jnp.bfloat16)
    wide = jnp.concatenate([attended[h * rows : (h + 1) * rows] for h in range(hs)], axis=1)
    acc_ref[...] += jnp.dot(wide, w_ref[...], preferred_element_type=jnp.float32)

    @pl.when(step == pl.num_programs(0) - 1)
    def _():
        half = out_refs[0].shape[1]
        parts = acc_ref.shape[1] // half
        tensor = slots // parts
        me = info_ref[nclips + 1]
        for slot in range(slots):
            to = lax.rem(me + slot, slots)
            row = pl.multiple_of(lax.rem(to, tensor) * moe_rows, moe_rows)
            if parts == 1:
                piece = acc_ref[pl.ds(row, moe_rows), :]
            else:
                column = pl.multiple_of(to // tensor * half, half)
                piece = acc_ref[pl.ds(row, moe_rows), pl.ds(column, half)]
            out_refs[slot][...] = piece.astype(out_refs[slot].dtype)


def attend(info, queries, kv_parts, w_out, nclips, slots, moe_rows, half):
    rows = queries.shape[0]
    heads = queries.shape[1] // HD
    hs = 2 if heads % 2 == 0 else 1
    lengths = tuple(part.shape[0] for part in kv_parts)
    whole = lambda g, info: (0, 0)
    return pl.pallas_call(
        functools.partial(attend_kernel, hs, lengths, nclips, slots, moe_rows),
        out_shape=[jax.ShapeDtypeStruct((moe_rows, half), jnp.bfloat16)] * slots,
        grid_spec=pltpu.PrefetchScalarGridSpec(
            num_scalar_prefetch=1,
            grid=(heads // hs,),
            in_specs=[pl.BlockSpec((rows, hs * HD), lambda g, info: (0, g))]
            + [pl.BlockSpec(part.shape, whole) for part in kv_parts]
            + [pl.BlockSpec((hs * HD, w_out.shape[1]), lambda g, info: (g, 0))],
            out_specs=[pl.BlockSpec((moe_rows, half), whole)] * slots,
            scratch_shapes=[
                pltpu.VMEM((rows, w_out.shape[1]), jnp.float32),
                pltpu.VMEM((rows, sum(lengths)), jnp.float32),
            ],
        ),
        name="attend",
    )(info, queries, *kv_parts, w_out)


def pack_kernel(count, experts, known, *refs):
    term_refs = refs[:count]
    residual_ref, gain_ref, ids_ref, mix_ref = refs[count : count + 4]
    refs = refs[count + 4 :]
    hidden = residual_ref[...].astype(jnp.float32)
    mixed = term_refs[0][...].astype(jnp.float32)
    for ref in term_refs[1:]:
        mixed = mixed + ref[...].astype(jnp.float32)
    hidden = hidden + mixed
    if known:
        squares, refs = refs[0][...], refs[1:]
    else:
        squares = jnp.sum(hidden * hidden, axis=1, keepdims=True)
    *packet_refs, hidden_ref = refs
    hidden_ref[...] = hidden
    rows, half = hidden.shape
    normed = (hidden * lax.rsqrt(squares / D + 1e-06) * gain_ref[...]).astype(jnp.bfloat16)
    width = packet_refs[0].shape[1] - half
    lane = lax.broadcasted_iota(jnp.int32, (rows, width), 1)
    share = jnp.zeros((rows, width), jnp.float32)
    for k in range(ids_ref.shape[1]):
        expert = ids_ref[:, k : k + 1]
        here = (lane == expert) | (lane == expert + experts)
        share = share + jnp.where(here, mix_ref[:, k : k + 1], 0.0)
    high = share.astype(jnp.bfloat16).astype(jnp.float32)
    tail = jnp.where(lane < experts, high, share - high).astype(jnp.bfloat16)
    count = rows // len(packet_refs)
    for index, ref in enumerate(packet_refs):
        ref[:, :half] = normed[index * count : (index + 1) * count]
        ref[:, half:] = tail[index * count : (index + 1) * count]


def pack(terms, residual, norm_gain, expert_ids, mix_weights, experts):
    rows, half = residual.shape
    width = -(-2 * experts // LANES) * LANES
    extra = []
    if lax.axis_size("pool") > 1:
        hidden = residual.astype(jnp.float32)
        hidden = hidden + sum(term.astype(jnp.float32) for term in terms)
        extra = [lax.psum(jnp.sum(hidden * hidden, axis=1, keepdims=True), "pool")]
    packet = jax.ShapeDtypeStruct((rows // CHUNKS, half + width), jnp.bfloat16)
    *packets, hidden_state = pl.pallas_call(
        functools.partial(pack_kernel, len(terms), experts, bool(extra)),
        out_shape=[packet] * CHUNKS + [jax.ShapeDtypeStruct((rows, half), jnp.float32)],
        compiler_params=SMALL,
        name="pack",
    )(*terms, residual, norm_gain[None, :], expert_ids, mix_weights, *extra)
    return packets, hidden_state


def join_kernel(*refs):
    *part_refs, out_ref = refs
    at = 0
    for ref in part_refs:
        count = ref.shape[0]
        out_ref[at : at + count, :] = ref[...]
        at += count


def joined(parts):
    if len(parts) == 1:
        return parts[0]
    shape = (sum(part.shape[0] for part in parts), parts[0].shape[1])
    return pl.pallas_call(
        join_kernel,
        out_shape=jax.ShapeDtypeStruct(shape, parts[0].dtype),
        compiler_params=SMALL,
        name="join",
    )(*parts)


def chosen_weight(tail, own, experts):
    lane = lax.broadcasted_iota(jnp.int32, tail.shape, 1)
    here = (lane == own) | (lane == own + experts)
    return jnp.sum(jnp.where(here, tail.astype(jnp.float32), 0.0), axis=1, keepdims=True)


def expert_kernel(count, experts, own_ref, *refs):
    part_refs = refs[:count]
    up_ref, down_ref = refs[count : count + 2]
    out_refs = refs[count + 2 :]
    half = out_refs[0].shape[1]
    ff = down_ref.shape[1]
    for part_ref, out_ref in zip(part_refs, out_refs):
        blended = 0.0
        for index in range(up_ref.shape[0]):
            both = jnp.dot(
                part_ref[:, :half], up_ref[index], preferred_element_type=jnp.float32
            )
            gate = both[:, :ff]
            hidden = (gate / (1.0 + jnp.exp(-gate)) * both[:, ff:]).astype(jnp.bfloat16)
            weight = chosen_weight(part_ref[:, half:], own_ref[0] + index, experts)
            result = jnp.dot(hidden, down_ref[index], preferred_element_type=jnp.float32)
            blended = blended + result * weight
        out_ref[...] = blended.astype(out_ref.dtype)


def run_experts(parts, w_gate_up, w_down, own, experts):
    half = w_down.shape[2]
    ff = w_down.shape[1]
    if lax.axis_size("pool") == 1:
        vmem = pl.BlockSpec(memory_space=pltpu.VMEM)
        return pl.pallas_call(
            functools.partial(expert_kernel, len(parts), experts),
            out_shape=[jax.ShapeDtypeStruct((p.shape[0], half), jnp.bfloat16) for p in parts],
            in_specs=[pl.BlockSpec(memory_space=pltpu.SMEM)] + [vmem] * (len(parts) + 2),
            out_specs=[vmem] * len(parts),
            compiler_params=LARGE,
            name="experts",
        )(own[None], *parts, w_gate_up, w_down)
    results = []
    for part in parts:
        blended = 0.0
        for index in range(w_gate_up.shape[0]):
            both = jnp.dot(part[:, :half], w_gate_up[index], preferred_element_type=jnp.float32)
            both = lax.psum(both.astype(jnp.bfloat16), "pool").astype(jnp.float32)
            hidden = (jax.nn.silu(both[:, :ff]) * both[:, ff:]).astype(jnp.bfloat16)
            weight = chosen_weight(part[:, half:], own + index, experts)
            result = jnp.dot(hidden, w_down[index], preferred_element_type=jnp.float32)
            blended = blended + result * weight
        results.append(blended.astype(jnp.bfloat16))
    return results


def body(
    queries,
    keys_values,
    residual,
    norm_gain,
    w_out,
    w_gate_up,
    w_down,
    expert_ids,
    mix_weights,
    clip_lengths,
):
    rows = queries.shape[0]
    heads_here = queries.shape[1] // HD
    moe_rows, half = residual.shape
    pool_size, tensor_size, context_size = (lax.axis_size(a) for a in ("pool", "tp", "ep"))
    pool_index, tensor_index, context_index = (lax.axis_index(a) for a in ("pool", "tp", "ep"))
    outer, inner = halves(context_size)
    tall, near = halves(tensor_size)
    sizes = (outer, inner, tall, near)
    mesh_axes = ("ep", "tp")

    def moved(value, dim, step, keep=None):
        pairs = shift_pairs(sizes, dim, step)
        if keep is not None:
            pairs = [pair for pair in pairs if keep(*pair)]
        return lax.ppermute(value, mesh_axes, pairs)

    pair_heads = keys_values.shape[1] // (2 * HD)
    head_pick = (
        pool_index * tensor_size + tensor_index
    ) * heads_here // (QH // KVH) - pool_index * pair_heads
    own_pairs = lax.dynamic_slice_in_dim(keys_values, head_pick * (2 * HD), 2 * HD, 1)
    longest = context_size * rows // 2

    def in_reach(source, target):
        apart = abs(source // (inner * tensor_size) - target // (inner * tensor_size))
        nearest = apart * inner - (inner - 1)
        return (nearest - 1) * rows + 1 < longest

    near_parts = [own_pairs]
    for step in range(1, outer):
        near_parts.append(moved(own_pairs, 0, -step, in_reach))
    kv_parts = [jnp.concatenate(near_parts, axis=0)]
    for step in range(1, inner):
        kv_parts.append(moved(kv_parts[0], 1, -step))
    outer_index, inner_index = context_index // inner, context_index % inner
    bases = [
        (((outer_index + a) % outer) * inner + (inner_index + b) % inner) * rows
        for b in range(inner)
        for a in range(outer)
    ]
    ends = jnp.cumsum(clip_lengths)
    slots = pool_size * tensor_size
    shard = pool_index * tensor_size + tensor_index
    info = jnp.concatenate(
        [ends, jnp.stack([context_index * rows, shard] + bases)]
    ).astype(jnp.int32)
    terms = attend(info, queries, kv_parts, w_out, ends.shape[0], slots, moe_rows, half)

    received = [terms[0]]
    for step in range(1, slots):
        pairs = [(source, (source + step) % slots) for source in range(slots)]
        received.append(lax.ppermute(terms[step], ("pool", "tp"), pairs))
    local_experts = w_gate_up.shape[0]
    experts = local_experts * context_size * tensor_size
    packets, hidden_state = pack(received, residual, norm_gain, expert_ids, mix_weights, experts)

    def pairs_of(phase, step):
        if phase in (1, 2) and inner == tall and near == 2:
            ways = [shift_pairs(sizes, phase, step), shift_pairs(sizes, 3 - phase, step)]
            return [pair for core in range(2) for pair in ways[core] if pair[0] % 2 == core]
        return shift_pairs(sizes, phase, step)

    def sent(value, phase, step):
        return lax.ppermute(value, mesh_axes, pairs_of(phase, step))

    own = (context_index * tensor_size + tensor_index) * local_experts
    outputs = []
    for index, value in enumerate(packets):
        for phase in range(3):
            value = joined(
                [value] + [sent(value, phase, -step) for step in range(1, sizes[phase])]
            )
        parts = [value] + [sent(value, 3, -step) for step in range(1, near)]
        results = run_experts(parts, w_gate_up, w_down, own, experts)
        total = results[0].astype(jnp.float32)
        for step in range(1, near):
            total = total + sent(results[step], 3, step).astype(jnp.float32)
        for phase in (2, 1, 0):
            count = total.shape[0] // sizes[phase]
            kept = total[:count]
            for step in range(1, sizes[phase]):
                piece = total[step * count : (step + 1) * count].astype(jnp.bfloat16)
                kept = kept + sent(piece, phase, step).astype(jnp.float32)
            total = kept
        count = total.shape[0]
        rest = hidden_state[index * count : (index + 1) * count]
        outputs.append((rest + total).astype(jnp.bfloat16))
    return jnp.concatenate(outputs, axis=0)


def solution(mesh):
    placed = (
        P(("grp", "ep"), ("pool", "tp")),
        P(("grp", "ep"), "pool"),
        P(("grp", "ep", "tp"), "pool"),
        P("pool"),
        P(("pool", "tp"), None),
        P(("ep", "tp"), "pool", None),
        P(("ep", "tp"), None, "pool"),
        P(("grp", "ep", "tp"), None),
        P(("grp", "ep", "tp"), None),
        P("grp"),
    )
    return jax.shard_map(
        body, mesh=mesh, in_specs=placed, out_specs=P(("grp", "ep", "tp"), "pool"), check_vma=False
    )
```
